32 devices in a mesh: dp: 16 (over z, x, core), mp: 2 (over y).
Axes of the slice: x: 2, y: 2, z: 4, core: 2. Of those that a mesh axis runs over, the one named last changes fastest.
Arguments:
- tokens: bfloat16 [16384, 768], P(('dp', 'mp')), may hold values from -6 to 6
- cotangent: bfloat16 [16384, 768], P(('dp', 'mp')), may hold values from -6 to 6
- lengths: int32 [80], P('dp'), may hold values from 0 to 512, as said below
- w_qkv: bfloat16 [768, 3, 768], P(None, None, 'mp'), may hold values from -0.21875 to 0.21875
- b_qv: float32 [2, 768], P(None, 'mp'), may hold values from -3 to 3
- w_out: bfloat16 [768, 768], P('mp'), may hold values from -1.75 to 1.75
- b_out: float32 [768], replicated, may hold values from -3 to 3
- gain_one: float32 [768], replicated, may hold values from 0.25 to 1.75
- shift_one: float32 [768], replicated, may hold values from -3 to 3
- w_up: bfloat16 [768, 3072], P(None, 'mp'), may hold values from -0.21875 to 0.21875
- b_up: float32 [3072], P('mp'), may hold values from -3 to 3
- w_down: bfloat16 [3072, 768], P('mp'), may hold values from -0.109375 to 0.109375
- b_down: float32 [768], replicated, may hold values from -3 to 3
- gain_two: float32 [768], replicated, may hold values from 0.25 to 1.75
- shift_two: float32 [768], replicated, may hold values from -3 to 3
Outputs:
- output: bfloat16 [16384, 768], P(('dp', 'mp'))
- grad_input: bfloat16 [16384, 768], P(('dp', 'mp'))
- grad_qkv: float32 [768, 3, 768], P('dp', None, 'mp')
- grad_qv_bias: float32 [2, 768], P(None, 'mp')
- grad_out_proj: float32 [768, 768], P('mp', 'dp')
- grad_out_bias: float32 [768], replicated
- grad_gain_one: float32 [768], replicated
- grad_shift_one: float32 [768], replicated
- grad_up: float32 [768, 3072], P('dp', 'mp')
- grad_up_bias: float32 [3072], P('mp')
- grad_down: float32 [3072, 768], P('mp', 'dp')
- grad_down_bias: float32 [768], replicated
- grad_gain_two: float32 [768], replicated
- grad_shift_two: float32 [768], replicated
- monitor: float32 [4], replicated
The draws below stay inside these ranges and needn't reach their ends.
Inputs may be any that keep to these rules, and one draw needn't show every extreme that they name: A row holds lengths real tokens at its start, 0 for an unused row; a used row holds at least half of its slots; every data index has at least one full short row, and some data index has a full long row.
All inputs are finite; a program needn't handle non-finite values.
Results may differ from the reference program's by a relative error of at most 0.02.
Values may be sent and summed in bfloat16 or wider, within the bound.
No kernel may reach another device: no remote copies, remote signals or barrier semaphores. Data moves between devices by JAX's collectives and lax.ppermute only.
A program may use at most 128 MiB of HBM per device.

```python
import jax
import jax.numpy as jnp
from jax import lax

D = 768
H = 12
HD = 64
FF = 3072
L_LONG = 512
L_SHORT = 128
R_LONG = 1
R_SHORT = 4
ROWS_DP = 5
TOK_DP = 1024
TOKENS = 16384
ROWS = 80
N_DP = 16


def draw_lengths(key, part):
    devices = ROWS // ROWS_DP
    span = max(devices - 1, 1)
    keys = jax.random.split(key, 5)
    place = jnp.arange(devices, dtype=jnp.int32)[:, None]
    column = jnp.arange(ROWS_DP, dtype=jnp.int32)[None, :]
    long_len = jax.random.randint(keys[0], (devices, R_LONG), L_LONG // 2, L_LONG + 1)
    short_len = jax.random.randint(keys[1], (devices, R_SHORT), L_SHORT // 2, L_SHORT + 1)
    sizes = jnp.concatenate([long_len, short_len], axis=1)
    roll = jax.random.randint(keys[2], (devices, ROWS_DP), 0, 3 * span)
    live = roll < span + 2 * place
    chosen = R_LONG + jax.random.randint(keys[3], (devices, 1), 0, R_SHORT)
    forced_short = column == chosen
    sizes = jnp.where(forced_short, L_SHORT, sizes)
    widest = jax.random.randint(keys[4], (), 0, devices)
    forced_long = (place == widest) & (column == 0)
    sizes = jnp.where(forced_long, L_LONG, sizes)
    live = live | forced_short | forced_long
    return jnp.where(live, sizes, 0).astype(jnp.int32).reshape(ROWS)


def block_levels(key, extent, shards, least, high):
    level, own = 1.0, jax.random.fold_in(key, 6)
    for axis_at, parts in shards:
        heights = jnp.exp(jax.random.uniform(jax.random.fold_in(own, axis_at), (parts,), jnp.float32, least / len(shards), high / len(shards)))
        level = level * jnp.repeat(heights, extent[axis_at] // parts).reshape([-1 if axis == axis_at else 1 for axis in range(len(extent))])
    return level


def gaussian(stream_key, extent, deviation, reach, pieces=(), held_as=jnp.bfloat16):
    result = deviation * jax.random.normal(stream_key, extent, jnp.float32)
    if pieces:
        result = result * block_levels(stream_key, extent, pieces, -0.22, 0.18)
    return jnp.clip(result, -reach, reach).astype(held_as)


def setup_inputs(seed: int = 0) -> dict:
    key_of = jax.random.split(jax.random.key(seed), 16)
    tokens = gaussian(key_of[0], (TOKENS, D), 1.0, 6.0, ((0, 32),))
    cotangent = gaussian(key_of[1], (TOKENS, D), 1.0, 6.0, ((0, 32),))
    lengths = draw_lengths(jax.random.fold_in(key_of[15], 71), 0)
    w_qkv = gaussian(key_of[3], (D, 3, D), D ** -0.5, 0.21875, ((2, 2),))
    b_qv = gaussian(key_of[4], (2, D), 0.5, 3.0, ((1, 2),), jnp.float32)
    w_out = gaussian(key_of[5], (D, D), (D // 64) ** -0.5, 1.75, ((0, 2),))
    b_out = gaussian(key_of[6], (D,), 0.5, 3.0, (), jnp.float32)
    gain_one = jnp.clip(1.0 + 0.15 * jax.random.normal(key_of[7], (D,), jnp.float32), 0.25, 1.75)
    shift_one = gaussian(key_of[8], (D,), 0.5, 3.0, (), jnp.float32)
    w_up = gaussian(key_of[9], (D, FF), D ** -0.5, 0.21875, ((1, 2),))
    b_up = gaussian(key_of[10], (FF,), 0.5, 3.0, ((0, 2),), jnp.float32)
    w_down = gaussian(key_of[11], (FF, D), FF ** -0.5, 0.109375, ((0, 2),))
    b_down = gaussian(key_of[12], (D,), 0.5, 3.0, (), jnp.float32)
    gain_two = jnp.clip(1.0 + 0.15 * jax.random.normal(key_of[13], (D,), jnp.float32), 0.25, 1.75)
    shift_two = gaussian(key_of[14], (D,), 0.5, 3.0, (), jnp.float32)
    return {"tokens": tokens, "cotangent": cotangent, "lengths": lengths, "w_qkv": w_qkv, "b_qv": b_qv, "w_out": w_out, "b_out": b_out, "gain_one": gain_one, "shift_one": shift_one, "w_up": w_up, "b_up": b_up, "w_down": w_down, "b_down": b_down, "gain_two": gain_two, "shift_two": shift_two}


@jax.custom_vjp
def low(v):
    return lax.optimization_barrier(v.astype(jnp.bfloat16)).astype(jnp.float32)

@jax.custom_vjp
def low_back(v):
    return v

def low_keep(v):
    return (low(v), None)

def low_pass(kept, grad):
    return (grad,)

def back_keep(v):
    return (v, None)

def back_low(kept, grad):
    return (low(grad),)
low.defvjp(low_keep, low_pass)
low_back.defvjp(back_keep, back_low)
EPS = 1e-12
HIGH = lax.Precision.HIGHEST

def rounded_both(value):
    return low(low_back(value))

def layer_norm(rows, gain, shift):
    mean = lax.optimization_barrier(jnp.mean(rows, axis=-1, keepdims=True))
    centred = rows - mean
    var = lax.optimization_barrier(jnp.mean(centred * centred, axis=-1, keepdims=True))
    return centred * lax.rsqrt(var + EPS) * gain + shift

def token_layout(lengths, total):
    place = jnp.arange(total, dtype=jnp.int32)
    long_span = R_LONG * L_LONG
    is_long = place < long_span
    row_long = place // L_LONG
    row_short = R_LONG + (place - long_span) // L_SHORT
    row = jnp.where(is_long, row_long, row_short).astype(jnp.int32)
    start = jnp.where(is_long, row_long * L_LONG, long_span + (row_short - R_LONG) * L_SHORT)
    offset = place - start
    table = jnp.arange(lengths.shape[0], dtype=jnp.int32)
    row_len = lax.optimization_barrier(jnp.sum(jnp.where(row[:, None] == table[None, :], lengths[None, :], 0), axis=1))
    return (row, offset < row_len)

def attend(query, keys, values, segment, valid):
    scale = query.shape[-1] ** (-0.5)
    allowed = (segment[:, None] == segment[None, :]) & valid[None, :]
    scores = low_back(jnp.einsum('qhd,khd->hqk', query, keys, precision=HIGH) * scale)
    scores = jnp.where(allowed[None], scores, -1e+30)
    probs = jax.nn.softmax(scores, axis=-1)
    return jnp.einsum('hqk,khd->qhd', low(probs), values, precision=HIGH)

def forward(params, tokens, segment, valid):
    w_qkv, b_qv, w_out, b_out, gain_one, shift_one, w_up, b_up, w_down, b_down, gain_two, shift_two = params
    count = tokens.shape[0]
    keep = valid.astype(tokens.dtype)[:, None]
    bias_rows = jnp.stack([b_qv[0], jnp.zeros_like(b_qv[0]), b_qv[1]])
    packed = rounded_both(jnp.einsum('td,dcf->tcf', tokens, w_qkv, precision=HIGH) + bias_rows)
    blocks = count // L_LONG
    shaped = packed.reshape(blocks, L_LONG, 3, H, HD)

    def one_block(items):
        block, seg, ok = items
        return attend(block[:, 0], block[:, 1], block[:, 2], seg, ok)
    mixed = lax.map(jax.checkpoint(one_block), (shaped, segment.reshape(blocks, L_LONG), valid.reshape(blocks, L_LONG)))
    mixed = rounded_both(mixed.reshape(count, D))
    branch = low_back(jnp.dot(mixed, w_out, precision=HIGH) + b_out)
    resid = tokens + branch
    normed = layer_norm(resid, gain_one, shift_one)
    hidden = low_back(jnp.dot(low(normed), w_up, precision=HIGH) + b_up)
    active = low(jax.nn.gelu(hidden, approximate=False))
    ffn = low_back(jnp.dot(active, w_down, precision=HIGH) + b_down)
    final = layer_norm(normed + ffn, gain_two, shift_two) * keep
    squares = jnp.stack([jnp.sum(keep * tokens * tokens), jnp.sum(keep * branch * branch), jnp.sum(keep * normed * normed), jnp.sum(keep * ffn * ffn)])
    return (final, (squares, jnp.sum(keep)))

def reference(tokens, cotangent, lengths, w_qkv, b_qv, w_out, b_out, gain_one, shift_one, w_up, b_up, w_down, b_down, gain_two, shift_two):
    params = tuple((item.astype(jnp.float32) for item in (w_qkv, b_qv, w_out, b_out, gain_one, shift_one, w_up, b_up, w_down, b_down, gain_two, shift_two)))
    token_blocks = tokens.astype(jnp.float32).reshape(N_DP, TOK_DP, D)
    grad_blocks = cotangent.astype(jnp.float32).reshape(N_DP, TOK_DP, D)
    length_blocks = lengths.reshape(N_DP, ROWS_DP)

    def step(carry, items):
        grads, squares, counted = carry
        block, grad_block, lens = items
        segment, valid = token_layout(lens, TOK_DP)

        def layer(weights, rows):
            return forward(weights, rows, segment, valid)
        final, back, aux = jax.vjp(layer, params, block, has_aux=True)
        grad_params, grad_rows = back(grad_block)
        grads = jax.tree.map(jnp.add, grads, grad_params)
        return ((grads, squares + aux[0], counted + aux[1]), (final.astype(jnp.bfloat16), grad_rows.astype(jnp.bfloat16)))
    zeros = jax.tree.map(jnp.zeros_like, params)
    start = (zeros, jnp.zeros((4,), jnp.float32), jnp.zeros((), jnp.float32))
    (grads, squares, counted), (finals, grad_rows) = lax.scan(step, start, (token_blocks, grad_blocks, length_blocks))
    monitor = jnp.sqrt(squares / (counted * D))
    return (finals.reshape(TOKENS, D), grad_rows.reshape(TOKENS, D), grads[0], grads[1], grads[2], grads[3], grads[4], grads[5], grads[6], grads[7], grads[8], grads[9], grads[10], grads[11], monitor)
```

```python
import functools

import jax
import jax.numpy as jnp
from jax import lax
from jax.experimental import pallas as pl
from jax.experimental.pallas import tpu as pltpu
from jax.sharding import PartitionSpec as P

D = 768
HD = 64
FF = 3072
L_LONG = 512
L_SHORT = 128
R_LONG = 1


EPS = 1e-12
BF16 = jnp.bfloat16
F32 = jnp.float32


def layer_norm(rows, gain, shift):
    mean = jnp.mean(rows, axis=-1, keepdims=True)
    centred = rows - mean
    var = jnp.mean(centred * centred, axis=-1, keepdims=True)
    return centred * lax.rsqrt(var + EPS) * gain + shift


def token_layout(lengths, total):
    place = jnp.arange(total, dtype=jnp.int32)
    long_span = R_LONG * L_LONG
    is_long = place < long_span
    row_long = place // L_LONG
    row_short = R_LONG + (place - long_span) // L_SHORT
    row = jnp.where(is_long, row_long, row_short)
    start = jnp.where(is_long, row_long * L_LONG, long_span + (row_short - R_LONG) * L_SHORT)
    offset = place - start
    table = jnp.arange(lengths.shape[0], dtype=jnp.int32)
    row_len = jnp.sum(jnp.where(row[:, None] == table[None, :], lengths[None, :], 0), axis=1)
    return (row, offset < row_len)


def contract(left, right, left_dim, right_dim, out=F32):
    return lax.dot_general(
        left, right, (((left_dim,), (right_dim,)), ((), ())), preferred_element_type=F32
    ).astype(out)


def mask_rows(code_ref, seg_ref, bias_ref):
    bias_ref[...] = jnp.where(code_ref[...] == seg_ref[...], 0.0, -1e30).astype(F32)


def attend_kernel(packed_ref, code_ref, seg_ref, mixed_ref, stat_ref, bias_ref, *, width):
    mask_rows(code_ref, seg_ref, bias_ref)

    def pair(at, _):
        col = pl.multiple_of(at * 2 * HD, 2 * HD)
        query = packed_ref[:, pl.ds(col, 2 * HD)]
        keys = packed_ref[:, pl.ds(width + col, 2 * HD)]
        values = packed_ref[:, pl.ds(2 * width + col, 2 * HD)]
        outs = []
        for half in range(2):
            part = slice(half * HD, (half + 1) * HD)
            scores = contract(keys[:, part], query[:, part] * HD**-0.5, 1, 1) + bias_ref[...]
            top = jnp.max(scores, axis=0, keepdims=True)
            weights = jnp.exp(scores - top)
            totals = jnp.sum(weights, axis=0, keepdims=True)
            out = contract(values[:, part], weights.astype(BF16), 0, 0) / totals
            outs.append(out)
            stat_ref[pl.ds(2 * at + half, 1), :] = top + jnp.log(totals)
        mixed_ref[:, pl.ds(col, 2 * HD)] = jnp.concatenate(outs, axis=0).T.astype(BF16)
        return 0

    lax.fori_loop(0, width // (2 * HD), pair, 0)


def attend_back_kernel(
    packed_ref, grad_ref, stat_ref, code_ref, seg_ref, out_ref, bias_ref, *, width
):
    mask_rows(code_ref, seg_ref, bias_ref)

    def pair(at, _):
        col = pl.multiple_of(at * 2 * HD, 2 * HD)
        query = packed_ref[:, pl.ds(col, 2 * HD)]
        keys = packed_ref[:, pl.ds(width + col, 2 * HD)]
        values = packed_ref[:, pl.ds(2 * width + col, 2 * HD)]
        grads = grad_ref[:, pl.ds(col, 2 * HD)]
        to_query, to_keys, to_values = [], [], []
        for half in range(2):
            part = slice(half * HD, (half + 1) * HD)
            scaled = query[:, part] * HD**-0.5
            scores = contract(keys[:, part], scaled, 1, 1) + bias_ref[...]
            probs = jnp.exp(scores - stat_ref[pl.ds(2 * at + half, 1), :])
            dprobs = contract(values[:, part], grads[:, part], 1, 1)
            product = probs * dprobs
            delta = jnp.sum(product, axis=0, keepdims=True)
            grad_scores = (product - probs * delta).astype(BF16)
            to_values.append(contract(probs.astype(BF16), grads[:, part], 1, 0))
            to_keys.append(contract(grad_scores, scaled, 1, 0))
            to_query.append(contract(keys[:, part], grad_scores, 0, 0) * HD**-0.5)
        out_ref[:, pl.ds(col, 2 * HD)] = jnp.concatenate(to_query, axis=0).T.astype(BF16)
        out_ref[:, pl.ds(width + col, 2 * HD)] = jnp.concatenate(to_keys, axis=1).astype(BF16)
        out_ref[:, pl.ds(2 * width + col, 2 * HD)] = jnp.concatenate(to_values, axis=1).astype(
            BF16
        )
        return 0

    lax.fori_loop(0, width // (2 * HD), pair, 0)


def attend(packed, code, seg):
    rows, width = packed.shape[0], packed.shape[1] // 3
    return pl.pallas_call(
        functools.partial(attend_kernel, width=width),
        out_shape=(
            jax.ShapeDtypeStruct((rows, width), BF16),
            jax.ShapeDtypeStruct((width // HD, rows), F32),
        ),
        scratch_shapes=[pltpu.VMEM((rows, rows), F32)],
        name="attend",
    )(packed, code, seg)


def attend_back(packed, grads, stat, code, seg):
    rows, width = packed.shape[0], packed.shape[1] // 3
    return pl.pallas_call(
        functools.partial(attend_back_kernel, width=width),
        out_shape=jax.ShapeDtypeStruct(packed.shape, BF16),
        scratch_shapes=[pltpu.VMEM((rows, rows), F32)],
        name="attend_back",
    )(packed, grads, stat, code, seg)


def across(value, bit):
    pairs = [(i, i ^ (1 << bit)) for i in range(lax.axis_size("dp"))]
    return lax.ppermute(value, "dp", pairs)


def swap(value):
    return lax.ppermute(value, "mp", [(0, 1), (1, 0)])


def bit_of(bit):
    return (lax.axis_index("dp") >> bit) & 1


def fetch(own):
    rows = own.shape[0] // 4
    core, side = bit_of(0), bit_of(1)
    first = swap(lax.dynamic_slice_in_dim(own, (core * 2 + side) * rows, rows, 0))
    second = across(first, 1)
    near = jnp.where(
        side == 0, jnp.concatenate([first, second]), jnp.concatenate([second, first])
    )
    far = across(near, 0)
    return jnp.where(core == 0, jnp.concatenate([near, far]), jnp.concatenate([far, near]))


def halve(value, bit, left):
    at = left.index(bit)
    high, low = 2**at, 2 ** (len(left) - at - 1)
    view = value.reshape(high, 2, low, *value.shape[1:])
    mine = bit_of(bit)
    got = across(lax.dynamic_index_in_dim(view, 1 - mine, 1, keepdims=False), bit)
    keep = lax.dynamic_index_in_dim(view, mine, 1, keepdims=False)
    total = (keep.astype(F32) + got.astype(F32)).reshape(high * low, *value.shape[1:])
    return total, [b for b in left if b != bit]


def low(value):
    return value.astype(BF16)


def reduce_grad(own, other):
    parts = lax.axis_size("dp")
    count = parts.bit_length() - 1
    left = list(range(count - 1, -1, -1))
    own = own.reshape(parts, D // parts, -1)
    other = other.reshape(parts, D // parts, -1)
    own, rest = halve(own, 0, left)
    other, _ = halve(other, 0, left)
    own, other = low(own), low(other)
    cut = -(-own.shape[-1] // 256) * 128
    one = own[..., :cut].astype(F32) + swap(other[..., :cut]).astype(F32)
    one, after = halve(low(one), 1, rest)
    two, _ = halve(own[..., cut:], 1, rest)
    two_other, _ = halve(other[..., cut:], 1, rest)
    two = low(two).astype(F32) + swap(low(two_other)).astype(F32)
    total = jnp.concatenate([one, two], axis=-1)
    for bit in range(2, count):
        total, after = halve(low(total), bit, after)
    return total.reshape(D // parts, -1)


def sum_all(value):
    value = value + swap(value)
    for bit in range(lax.axis_size("dp").bit_length() - 1):
        value = value + across(value, bit)
    return value


def gelu_both(hidden):
    cdf = 0.5 * (1.0 + lax.erf(hidden * (0.5**0.5)))
    slope = cdf + hidden * jnp.exp(-0.5 * hidden * hidden) * (0.5 / jnp.pi) ** 0.5
    return low(hidden * cdf), low(slope)


def place_halves(own, other, mine):
    return jnp.where(
        mine == 0,
        jnp.concatenate([own, other], axis=-1),
        jnp.concatenate([other, own], axis=-1),
    )


def shards(
    tokens,
    cotangent,
    lengths,
    w_qkv,
    b_qv,
    w_out,
    b_out,
    gain_one,
    shift_one,
    w_up,
    b_up,
    w_down,
    b_down,
    gain_two,
    shift_two,
):
    rows = tokens.shape[0]
    total = rows * lax.axis_size("mp")
    mine = lax.axis_index("mp")
    width = w_qkv.shape[2]
    units = w_up.shape[1]
    segment, valid = token_layout(lengths, total)
    segment = lax.dynamic_slice_in_dim(segment, mine * rows, rows)
    valid = lax.dynamic_slice_in_dim(valid, mine * rows, rows)
    keep = valid.astype(F32)[:, None]
    code = jnp.where(valid, segment, -1)[:, None]
    seg = segment[None, :]

    w_qkv = w_qkv.reshape(D, 3 * width)
    small = swap(jnp.concatenate([b_qv[0], b_qv[1], b_up])[None])[0]
    qv_bias = [b_qv, small[: 2 * width].reshape(2, width)]
    up_bias = [b_up, small[2 * width :]]
    qkv = [w_qkv, fetch(w_qkv)]
    out = [w_out, fetch(w_out)]
    up = [w_up, fetch(w_up)]
    down = [w_down, fetch(w_down)]

    packed, mixed, stats = [], [], []
    for half in range(2):
        bias = jnp.concatenate([qv_bias[half][0], jnp.zeros((width,), F32), qv_bias[half][1]])
        packed.append(low(contract(tokens, qkv[half], 1, 0) + bias))
        mix, stat = attend(packed[half], code, seg)
        mixed.append(mix)
        stats.append(stat)
    branch = contract(mixed[0], out[0], 1, 0) + contract(mixed[1], out[1], 1, 0) + b_out
    wide = tokens.astype(F32)
    resid = wide + branch
    normed = layer_norm(resid, gain_one, shift_one)
    normed_low = low(normed)
    active, slope = [], []
    for half in range(2):
        act, slo = gelu_both(contract(normed_low, up[half], 1, 0) + up_bias[half])
        active.append(act)
        slope.append(slo)
    ffn = contract(active[0], down[0], 1, 0) + contract(active[1], down[1], 1, 0) + b_down
    second = normed + ffn
    final_out = low(layer_norm(second, gain_two, shift_two) * keep)
    squares = [jnp.sum(keep * v * v) for v in (wide, branch, normed, ffn)]
    grad_final = cotangent.astype(F32) * keep
    _, norm_two_back = jax.vjp(layer_norm, second, gain_two, shift_two)
    grad_second, grad_gain_two, grad_shift_two = norm_two_back(grad_final)
    grad_ffn = low(grad_second)
    grad_down = reduce_grad(
        contract(grad_ffn, active[0], 0, 0, BF16), contract(grad_ffn, active[1], 0, 0, BF16)
    )
    grad_hidden = [
        low(contract(grad_ffn, down[half], 1, 1) * slope[half].astype(F32)) for half in range(2)
    ]
    grad_up = reduce_grad(
        contract(normed_low, grad_hidden[0], 0, 0, BF16),
        contract(normed_low, grad_hidden[1], 0, 0, BF16),
    )
    grad_normed = (
        grad_second + contract(grad_hidden[0], up[0], 1, 1) + contract(grad_hidden[1], up[1], 1, 1)
    )
    _, norm_one_back = jax.vjp(layer_norm, resid, gain_one, shift_one)
    grad_resid, grad_gain_one, grad_shift_one = norm_one_back(grad_normed)
    grad_branch = low(grad_resid)
    grad_out = reduce_grad(
        contract(grad_branch, mixed[0], 0, 0, BF16), contract(grad_branch, mixed[1], 0, 0, BF16)
    )
    grad_packed = [
        attend_back(
            packed[half], contract(grad_branch, out[half], 1, 1, BF16), stats[half], code, seg
        )
        for half in range(2)
    ]
    grad_qkv = reduce_grad(
        contract(tokens, grad_packed[0], 0, 0, BF16), contract(tokens, grad_packed[1], 0, 0, BF16)
    )
    grad_input = low(
        grad_resid
        + contract(grad_packed[0], qkv[0], 1, 1)
        + contract(grad_packed[1], qkv[1], 1, 1)
    )

    def sums(array):
        return jnp.sum(array, axis=0, dtype=F32)

    totals = [sums(item) for item in grad_packed]
    pieces = [
        grad_gain_one,
        grad_shift_one,
        grad_gain_two,
        grad_shift_two,
        sums(grad_branch),
        sums(grad_ffn),
        place_halves(totals[0][:width], totals[1][:width], mine),
        place_halves(totals[0][2 * width :], totals[1][2 * width :], mine),
        place_halves(sums(grad_hidden[0]), sums(grad_hidden[1]), mine),
        jnp.stack([*squares, jnp.sum(keep)]),
    ]
    flat = jnp.concatenate(pieces)
    flat = jnp.pad(flat, (0, -flat.shape[0] % 1024)).reshape(8, -1)
    flat = sum_all(flat).reshape(-1)
    rows_sum = flat[: 8 * D].reshape(8, D)
    up_sum = flat[8 * D : 8 * D + FF]
    tail = flat[8 * D + FF : 8 * D + FF + 5]
    monitor = jnp.sqrt(tail[:4] / (tail[4] * D))
    return (
        final_out,
        grad_input,
        grad_qkv.reshape(-1, 3, width),
        lax.dynamic_slice_in_dim(rows_sum[6:8], mine * width, width, 1),
        grad_out.T,
        rows_sum[4],
        rows_sum[0],
        rows_sum[1],
        grad_up,
        lax.dynamic_slice_in_dim(up_sum, mine * units, units, 0),
        grad_down.T,
        rows_sum[5],
        rows_sum[2],
        rows_sum[3],
        monitor,
    )


def solution(mesh):
    return jax.shard_map(
        shards,
        mesh=mesh,
        in_specs=(
            P(("dp", "mp"), None),
            P(("dp", "mp"), None),
            P("dp"),
            P(None, None, "mp"),
            P(None, "mp"),
            P("mp", None),
            P(),
            P(),
            P(),
            P(None, "mp"),
            P("mp"),
            P("mp", None),
            P(),
            P(),
            P(),
        ),
        out_specs=(
            P(("dp", "mp"), None),
            P(("dp", "mp"), None),
            P("dp", None, "mp"),
            P(None, "mp"),
            P("mp", "dp"),
            P(),
            P(),
            P(),
            P("dp", "mp"),
            P("mp"),
            P("mp", "dp"),
            P(),
            P(),
            P(),
            P(),
        ),
        check_vma=False,
    )
```
